256 devices in a mesh: req: 64 (over z, x, core), ffn: 4 (over y).
Axes of the slice: x: 4, y: 4, z: 8, core: 2. Of those that a mesh axis runs over, the one named last changes fastest.
Arguments:
- residual: bfloat16 [16384, 2048], P('req')
- queries: bfloat16 [16384, 4096], P('req', 'ffn')
- rotated_key_rows: bfloat16 [16384, 2048], P('req', 'ffn')
- values: bfloat16 [16384, 2048], P('req', 'ffn'), may hold values from -6 to 6
- req_start: int32 [16384], P('req'), may hold values from 0 to 16383, as said below
- head_sink_logit: float32 [32], P('ffn'), may hold values from 6 to 11
- out_proj: bfloat16 [4096, 2048], P('ffn', 'req'), may hold values from -0.25 to 0.25
- mid_gain: float32 [2048], replicated, may hold values from 0.1 to 1.9
- router_logits: float32 [16384, 8], P('req')
- routes: int32 [16384, 2], P('req'), may hold values from 0 to 63, as said below
- placement: int32 [64], replicated, may hold values from 0 to 7, as said below
- w_gate: bfloat16 [64, 2048, 3072], P('req', None, 'ffn'), as said below
- w_up: bfloat16 [64, 2048, 3072], P('req', None, 'ffn'), as said below
- w_down: bfloat16 [64, 2048, 3072], P('req', None, 'ffn'), as said below
Outputs:
- layer_out: bfloat16 [16384, 2048], P('req', 'ffn')
The draws below stay inside these ranges and needn't reach their ends.
Inputs may be any that keep to these rules, and one draw needn't show every extreme that they name: req_start[p] is the first position of the request that holds position p; requests are runs of consecutive positions, each at most 8192 long, one is exactly 8192 long, and the last position is a request of one token. `routes`: the two entries of a token name indices that host different experts. Among the 512 entries of the tokens of one index of req, an index appears at most 10 times, and every index that hosts one certain expert appears exactly 10 times, in every such block. `placement`: every expert is hosted at one index or more. `w_gate`: rows k and m are equal where placement[k] == placement[m]. `w_up`: rows k and m are equal where placement[k] == placement[m]. `w_down`: rows k and m are equal where placement[k] == placement[m].
All inputs are finite; a program needn't handle non-finite values.
Results may differ from the reference program's by a relative error of at most 0.0075.
Values may be sent and summed in bfloat16 or wider, within the bound.
A program may use at most 128 MiB of HBM per device.

```python
import math
import jax
import jax.numpy as jnp
from jax import lax

D = 2048
QUERY_HEADS = 32
KEY_VALUE_HEADS = 16
HEAD_SIZE = 128
EXPERTS = 8
FF = 3072
TOKENS_PER_SHARD = 256
TOTAL_TOKENS = 16384
WINDOW_TOKENS = 4096
MAXLEN = 8192
CAP = 10
N_REQ = 64
N_FFN = 4


def folded_random_key(key, number):
    return jax.random.fold_in(key, number)


def base_keys(key):
    return jnp.clip(jax.random.normal(folded_random_key(key, 22), (TOTAL_TOKENS, KEY_VALUE_HEADS * HEAD_SIZE), jnp.float32), -5.0, 5.0) * 1.6


def draw_residual(key, part):
    log_low = math.log(0.3)
    log_high = math.log(3.0)
    col_scale = jnp.exp(jax.random.uniform(folded_random_key(key, 41), (1, D), jnp.float32, log_low, log_high))
    row_scale = jnp.exp(jax.random.uniform(folded_random_key(key, 42), (TOTAL_TOKENS, 1), jnp.float32, log_low, log_high))
    base_draw = jnp.clip(jax.random.normal(folded_random_key(key, 43), (TOTAL_TOKENS, D), jnp.float32), -4.0, 4.0)
    return (base_draw * row_scale * col_scale).astype(jnp.bfloat16)


def draw_rotated_key_rows(key, part):
    starting_keys = base_keys(key)
    return starting_keys.astype(jnp.bfloat16)


def draw_queries(key, part):
    query_draw = jnp.clip(jax.random.normal(folded_random_key(key, 23), (TOTAL_TOKENS, QUERY_HEADS * HEAD_SIZE), jnp.float32), -5.0, 5.0) * 1.6
    return query_draw.astype(jnp.bfloat16)


def draw_router_logits(key, part):
    logits = jnp.clip(jax.random.normal(folded_random_key(key, 31), (TOTAL_TOKENS, EXPERTS), jnp.float32), -6.0, 6.0) * 2.0
    return logits


def host_table(key):
    profile = jnp.array([4, 3, 2, 2, 2, 1, 1, 1], jnp.int32)
    extra_slots = N_REQ - EXPERTS
    extra_quota = extra_slots * profile // 16
    leftover = extra_slots - jnp.sum(extra_quota)
    host_counts = 1 + extra_quota + (jnp.arange(EXPERTS) < leftover).astype(jnp.int32)
    hot_order = jax.random.permutation(folded_random_key(key, 51), EXPERTS)
    by_expert = jnp.zeros((EXPERTS,), jnp.int32).at[hot_order].set(host_counts)
    host_ends = jnp.cumsum(by_expert)
    slot_ids = jnp.arange(N_REQ)
    unsorted = jnp.sum((slot_ids[:, None] >= host_ends[None, :]).astype(jnp.int32), axis=1)
    shuffle = jax.random.permutation(folded_random_key(key, 52), N_REQ)
    return unsorted[shuffle].astype(jnp.int32)


def draw_placement(key, part):
    return host_table(key)


def placed_weights(key, number, fan_in):
    base_draw = jnp.clip(jax.random.normal(folded_random_key(key, number), (EXPERTS, D, FF), jnp.float32), -6.0, 6.0) * fan_in ** (-0.5)
    return jnp.take(base_draw, host_table(key), axis=0).astype(jnp.bfloat16)


def draw_w_gate(key, part):
    return placed_weights(key, 71, D)


def draw_w_up(key, part):
    return placed_weights(key, 72, D)


def draw_w_down(key, part):
    return placed_weights(key, 73, FF)


def draw_routes(key, part):
    hosts = host_table(key)
    tickets = N_REQ * CAP
    ticket_ids = jnp.arange(tickets, dtype=jnp.int32)
    ticket_dest = ticket_ids // CAP
    ticket_expert = hosts[ticket_dest]
    heavy_expert = jax.random.randint(folded_random_key(key, 53), (), 0, EXPERTS)

    def one_block(block_key):
        noise_draw = jax.random.randint(block_key, (tickets,), 0, 1 << 16)
        ticket_score = noise_draw * tickets + ticket_ids
        ticket_score = jnp.where(ticket_expert == heavy_expert, ticket_score - (1 << 16) * tickets, ticket_score)
        picked = jnp.argsort(ticket_score)[:2 * TOKENS_PER_SHARD]
        picked_expert = ticket_expert[picked]
        ranking = jnp.argsort(picked_expert * tickets + picked)
        ranked = ticket_dest[picked[ranking]]
        first = ranked[:TOKENS_PER_SHARD]
        second = ranked[TOKENS_PER_SHARD:]
        flip_pair = jax.random.randint(folded_random_key(block_key, 1), (TOKENS_PER_SHARD,), 0, 2) == 1
        paired = jnp.stack([jnp.where(flip_pair, second, first), jnp.where(flip_pair, first, second)], axis=1)
        shuffle = jax.random.permutation(folded_random_key(block_key, 2), TOKENS_PER_SHARD)
        return paired[shuffle]
    keys_in_block = jax.vmap(lambda index_value: jax.random.fold_in(folded_random_key(key, 54), index_value))(jnp.arange(N_REQ))
    return jax.vmap(one_block)(keys_in_block).reshape(TOTAL_TOKENS, 2).astype(jnp.int32)


def draw_req_start(key, part):
    positions = jnp.arange(TOTAL_TOKENS, dtype=jnp.int32)
    offset = jax.random.randint(folded_random_key(key, 61), (), 0, MAXLEN)
    full_count = (TOTAL_TOKENS - 1 - offset) // MAXLEN
    chosen = jax.random.randint(folded_random_key(key, 62), (), 0, full_count)
    low_edge = offset + chosen * MAXLEN
    extra_cuts = jax.random.randint(folded_random_key(key, 63), (TOTAL_TOKENS,), 0, 512) == 0
    guarded = (positions > low_edge) & (positions < low_edge + MAXLEN)
    is_start = (positions == 0) | (positions == TOTAL_TOKENS - 1) | ((positions - offset) % MAXLEN == 0) | extra_cuts & jnp.logical_not(guarded)
    marked = jnp.where(is_start, positions, 0)
    return lax.cummax(marked, axis=0).astype(jnp.int32)


def shard_levels(key, extent, split, least, high):
    level = 1.0
    for dim, blocks in split:
        heights = jax.random.uniform(jax.random.fold_in(jax.random.fold_in(key, 6), dim), (blocks,), jnp.float32, least / len(split), high / len(split))
        level = level * jnp.repeat(jnp.exp(heights), extent[dim] // blocks).reshape((-1,) + (1,) * (len(extent) - 1 - dim))
    return level


def centred(own_key, shape, width, most, pieces=(), kind=jnp.bfloat16):
    entries = width * jax.random.normal(own_key, shape, jnp.float32)
    if pieces:
        entries = entries * shard_levels(own_key, shape, pieces, -0.22, 0.18)
    return jnp.clip(entries, -most, most).astype(kind)


def setup_inputs(seed: int = 0) -> dict:
    key_of = jax.random.split(jax.random.key(seed), 15)
    return {
        "residual": draw_residual(jax.random.fold_in(key_of[14], 71), 0),
        "queries": draw_queries(jax.random.fold_in(key_of[14], 71), 0),
        "rotated_key_rows": draw_rotated_key_rows(jax.random.fold_in(key_of[14], 71), 0),
        "values": centred(key_of[3], (TOTAL_TOKENS, KEY_VALUE_HEADS * HEAD_SIZE), 1.0, 6.0, ((0, 64), (1, 4))),
        "req_start": draw_req_start(jax.random.fold_in(key_of[14], 71), 0),
        "head_sink_logit": jnp.clip(6.0 + 5.0 * jax.random.uniform(key_of[5], (QUERY_HEADS,), jnp.float32) ** shard_levels(key_of[5], (QUERY_HEADS,), ((0, 4),), -0.2, 0.2), 6.0, 11.0),
        "out_proj": centred(key_of[6], (QUERY_HEADS * HEAD_SIZE, D), (QUERY_HEADS * HEAD_SIZE // 8) ** -0.5, 0.25, ((0, 4), (1, 64))),
        "mid_gain": jnp.clip(1.0 + 0.18 * jax.random.normal(key_of[7], (D,), jnp.float32), 0.1, 1.9),
        "router_logits": draw_router_logits(jax.random.fold_in(key_of[14], 71), 0),
        "routes": draw_routes(jax.random.fold_in(key_of[14], 71), 0),
        "placement": draw_placement(jax.random.fold_in(key_of[14], 71), 0),
        "w_gate": draw_w_gate(jax.random.fold_in(key_of[14], 71), 0),
        "w_up": draw_w_up(jax.random.fold_in(key_of[14], 71), 0),
        "w_down": draw_w_down(jax.random.fold_in(key_of[14], 71), 0),
    }


EPS = 1e-06
block_rows = 128

def attention(queries, rotated_key_rows, values, req_start, head_sink_logit):
    query_group_width = QUERY_HEADS // KEY_VALUE_HEADS
    logit_scale_factor = HEAD_SIZE ** (-0.5)
    leading_zero_rows = jnp.zeros((WINDOW_TOKENS, KEY_VALUE_HEADS * HEAD_SIZE), rotated_key_rows.dtype)
    gathered_keys = jnp.concatenate([leading_zero_rows, rotated_key_rows], axis=0)
    gathered_values = jnp.concatenate([leading_zero_rows, values], axis=0)
    key_range_length = WINDOW_TOKENS + TOKENS_PER_SHARD
    initial_sink_logit = head_sink_logit.reshape(KEY_VALUE_HEADS, query_group_width, 1)

    def one_block(block_index):
        leading_row = block_index * TOKENS_PER_SHARD
        queries_in_block = lax.dynamic_slice_in_dim(queries, leading_row, TOKENS_PER_SHARD, 0).astype(jnp.float32).reshape(TOKENS_PER_SHARD, KEY_VALUE_HEADS, query_group_width, HEAD_SIZE)
        keys_in_block = lax.dynamic_slice_in_dim(gathered_keys, leading_row, key_range_length, 0).astype(jnp.float32).reshape(key_range_length, KEY_VALUE_HEADS, HEAD_SIZE)
        values_in_block = lax.dynamic_slice_in_dim(gathered_values, leading_row, key_range_length, 0).astype(jnp.float32).reshape(key_range_length, KEY_VALUE_HEADS, HEAD_SIZE)
        starts = lax.dynamic_slice_in_dim(req_start, leading_row, TOKENS_PER_SHARD, 0)
        query_pos = leading_row + jnp.arange(TOKENS_PER_SHARD, dtype=jnp.int32)
        key_pos = leading_row - WINDOW_TOKENS + jnp.arange(key_range_length, dtype=jnp.int32)
        visible = (key_pos[None, :] >= starts[:, None]) & (key_pos[None, :] <= query_pos[:, None]) & (query_pos[:, None] - key_pos[None, :] < WINDOW_TOKENS)
        attention_logits = jnp.einsum('veck,uek->ecvu', queries_in_block, keys_in_block) * logit_scale_factor
        attention_logits = jnp.where(visible[None, None], attention_logits, -jnp.inf)
        row_peak = jnp.maximum(lax.optimization_barrier(jnp.max(attention_logits, axis=-1)), initial_sink_logit)
        probs = jnp.exp(attention_logits - row_peak[..., None])
        row_total = lax.optimization_barrier(jnp.sum(probs, axis=-1)) + jnp.exp(initial_sink_logit - row_peak)
        reduced_probabilities = lax.optimization_barrier(probs.astype(jnp.bfloat16)).astype(jnp.float32)
        weighted_value_sum = jnp.einsum('plyw,wpj->plyj', reduced_probabilities, values_in_block)
        result = weighted_value_sum / row_total[..., None]
        return jnp.transpose(result, (2, 0, 1, 3)).reshape(TOKENS_PER_SHARD, QUERY_HEADS * HEAD_SIZE).astype(jnp.bfloat16)
    blocks = lax.map(one_block, jnp.arange(TOTAL_TOKENS // TOKENS_PER_SHARD, dtype=jnp.int32))
    return blocks.reshape(TOTAL_TOKENS, QUERY_HEADS * HEAD_SIZE)

def expert_outputs(normed, hosts_flat, w_gate, w_up, w_down):
    row_count = hosts_flat.shape[0]
    group_count = N_REQ
    by_host = jnp.argsort(hosts_flat, stable=True).astype(jnp.int32)
    host_hot = (hosts_flat[:, None] == jnp.arange(group_count, dtype=jnp.int32)[None, :]).astype(jnp.int32)
    counts = lax.optimization_barrier(jnp.sum(host_hot, axis=0))
    padded = (counts + block_rows - 1) // block_rows * block_rows
    pad_start = jnp.cumsum(padded) - padded
    plain_start = jnp.cumsum(counts) - counts
    sorted_ids = hosts_flat[by_host]
    slot_of = pad_start[sorted_ids] + jnp.arange(row_count, dtype=jnp.int32) - plain_start[sorted_ids]
    capacity = (row_count + block_rows - 1) // block_rows * block_rows + group_count * block_rows
    buffer = jnp.zeros((capacity, D), normed.dtype).at[slot_of].set(normed[by_host // 2])
    block_count = capacity // block_rows
    block_first = jnp.arange(block_count, dtype=jnp.int32) * block_rows
    block_host = jnp.minimum(lax.optimization_barrier(jnp.sum((block_first[:, None] >= (pad_start + padded)[None, :]).astype(jnp.int32), axis=1)), group_count - 1)
    quarter = FF // N_FFN

    def one_block(operands):
        block_in, host = operands
        inputs = block_in.astype(jnp.float32)
        gate_val = jnp.dot(inputs, w_gate[host].astype(jnp.float32), preferred_element_type=jnp.float32)
        up_val = jnp.dot(inputs, w_up[host].astype(jnp.float32), preferred_element_type=jnp.float32)
        activated = (jax.nn.silu(gate_val) * up_val).astype(jnp.bfloat16).astype(jnp.float32)
        down_mat = w_down[host].astype(jnp.float32)
        summed = jnp.zeros((block_rows, D), jnp.float32)
        for piece_idx in range(N_FFN):
            low_cols = piece_idx * quarter
            piece = jnp.dot(activated[:, low_cols:low_cols + quarter], down_mat[:, low_cols:low_cols + quarter].T, preferred_element_type=jnp.float32)
            piece = lax.optimization_barrier(piece.astype(jnp.bfloat16))
            summed = summed + piece.astype(jnp.float32)
        return summed
    results = lax.map(one_block, (buffer.reshape(block_count, block_rows, D), block_host))
    gathered = results.reshape(capacity, D)[slot_of]
    return jnp.zeros((row_count, D), jnp.float32).at[by_host].set(gathered)

def reference(residual, queries, rotated_key_rows, values, req_start, head_sink_logit, out_proj, mid_gain, router_logits, routes, placement, w_gate, w_up, w_down):
    attended = attention(queries, rotated_key_rows, values, req_start, head_sink_logit)
    proj = jnp.dot(attended.astype(jnp.float32), out_proj.astype(jnp.float32), preferred_element_type=jnp.float32)
    hidden = residual.astype(jnp.float32) + proj
    mean_sq = lax.optimization_barrier(jnp.mean(hidden * hidden, axis=1, keepdims=True))
    normed = (hidden * lax.rsqrt(mean_sq + EPS) * mid_gain).astype(jnp.bfloat16)
    expert_of = placement[routes]
    expert_hot = (expert_of[:, :, None] == jnp.arange(EXPERTS, dtype=jnp.int32)[None, None, :]).astype(jnp.float32)
    chosen = lax.optimization_barrier(jnp.sum(router_logits[:, None, :] * expert_hot, axis=2))
    logit_peak = lax.optimization_barrier(jnp.max(chosen, axis=1, keepdims=True))
    exp_logits = jnp.exp(chosen - logit_peak)
    gate_weights = exp_logits / lax.optimization_barrier(jnp.sum(exp_logits, axis=1, keepdims=True))
    outputs = expert_outputs(normed, routes.reshape(-1).astype(jnp.int32), w_gate, w_up, w_down).reshape(TOTAL_TOKENS, 2, D)
    mixture = lax.optimization_barrier(jnp.sum(outputs * gate_weights[:, :, None], axis=1))
    return (hidden + mixture).astype(jnp.bfloat16)
```

```python
import jax
import jax.numpy as jnp
from jax import lax
from jax.experimental import pallas as pl
from jax.experimental.pallas import tpu as pltpu
from jax.sharding import PartitionSpec as P

QUERY_HEADS = 32
KEY_VALUE_HEADS = 16
HEAD_SIZE = 128
EXPERTS = 8


EPS = 1e-06


def shifted(value, axis, steps):
    count = lax.axis_size(axis)
    initial, last = (max(0, -steps), min(count, count - steps))
    return lax.ppermute(value, axis, [(source, source + steps) for source in range(initial, last)])


def step_back(keys_in_block, values_in_block):
    return shifted((keys_in_block, values_in_block), "req", 1)


MESH = pl.DeviceIdType.MESH
ROW_TILE = 128


def greet_group(size):
    me = lax.axis_index("ffn")
    barrier = pltpu.get_barrier_semaphore()
    for d in range(1, size):
        pl.semaphore_signal(
            barrier, inc=1, device_id={"ffn": lax.rem(me + d, size)}, device_id_type=MESH
        )
    pl.semaphore_wait(barrier, size - 1)
    return me


def send(src, dst, send_sem, recv_sem, peer):
    copy = pltpu.make_async_remote_copy(
        src_ref=src,
        dst_ref=dst,
        send_sem=send_sem,
        recv_sem=recv_sem,
        device_id={"ffn": peer},
        device_id_type=MESH,
    )
    copy.start()
    return copy


def norm_kernel(size, proj_ref, res_ref, gain_ref, hidden_ref, normed_ref, landed, own_sq, peer_sq, s1, r1, s2, r2):
    width = proj_ref.shape[1]
    quarter = width // size
    me = greet_group(size)
    copies = []
    for d in range(1, size):
        peer = lax.rem(me + d, size)
        cols = pl.ds(pl.multiple_of(peer * quarter, quarter), quarter)
        copies.append(send(proj_ref.at[:, cols], landed.at[d - 1], s1.at[d - 1], r1.at[d - 1], peer))
    own = pl.ds(pl.multiple_of(me * quarter, quarter), quarter)
    hidden_ref[...] = proj_ref[:, own].astype(jnp.float32)
    for d in (1, 3, 2):
        copies[d - 1].wait()
        hidden_ref[...] += landed[d - 1].astype(jnp.float32)
    hidden = hidden_ref[...] + res_ref[:, own].astype(jnp.float32)
    hidden_ref[...] = hidden
    sq = jnp.sum(hidden * hidden, axis=1, keepdims=True)
    own_sq[...] = jnp.broadcast_to(sq, own_sq.shape)
    copies = []
    for d in range(1, size):
        peer = lax.rem(me + d, size)
        copies.append(send(own_sq, peer_sq.at[d - 1], s2.at[d - 1], r2.at[d - 1], peer))
    for copy in copies:
        copy.wait()
    total = own_sq[...]
    for d in range(1, size):
        total = total + peer_sq[d - 1]
    scale = lax.rsqrt(total[:, :1] * (1.0 / width) + EPS)
    normed_ref[...] = (hidden_ref[...] * scale * gain_ref[:, own]).astype(jnp.bfloat16)


def norm_call(size, proj, residual, mid_gain):
    rows, width = proj.shape
    quarter = width // size
    vmem = pl.BlockSpec(memory_space=pltpu.VMEM)
    dma = pltpu.SemaphoreType.DMA((size - 1,))
    return pl.pallas_call(
        lambda *refs: norm_kernel(size, *refs),
        out_shape=(
            jax.ShapeDtypeStruct((rows, quarter), jnp.float32),
            jax.ShapeDtypeStruct((rows, quarter), jnp.bfloat16),
        ),
        in_specs=[vmem] * 3,
        out_specs=(vmem, vmem),
        scratch_shapes=[
            pltpu.VMEM((size - 1, rows, quarter), jnp.bfloat16),
            pltpu.VMEM((rows, 128), jnp.float32),
            pltpu.VMEM((size - 1, rows, 128), jnp.float32),
            dma,
            dma,
            dma,
            dma,
        ],
        compiler_params=pltpu.CompilerParams(collective_id=1, has_side_effects=True),
        name="norm_exchange",
    )(proj, residual, mid_gain)


def expert_kernel(
    size, x_ref, gate_hbm, up_hbm, down_hbm, out_ref,
    gate_mat, up_mat, down_mat, wide, gate_acc, up_acc, act, parts, landed,
    wsem, s1, r1, s2, r2,
):
    rows, quarter = x_ref.shape
    loads = [
        pltpu.make_async_copy(gate_hbm, gate_mat, wsem.at[0]),
        pltpu.make_async_copy(up_hbm, up_mat, wsem.at[1]),
        pltpu.make_async_copy(down_hbm, down_mat, wsem.at[2]),
    ]
    for load in loads:
        load.start()
    me = greet_group(size)
    copies = []
    for d in range(1, size):
        peer = lax.rem(me + d, size)
        copies.append(send(x_ref, wide.at[d - 1], s1.at[d - 1], r1.at[d - 1], peer))
    loads[0].wait()
    loads[1].wait()
    tiles = rows // ROW_TILE

    def tile_rows(tile):
        return pl.ds(pl.multiple_of(tile * ROW_TILE, ROW_TILE), ROW_TILE)

    for d in (0, 1, 3, 2):
        if d:
            copies[d - 1].wait()
        source = lax.rem(me + size - d, size)
        k_rows = pl.ds(pl.multiple_of(source * quarter, quarter), quarter)

        def one(tile, carry, d=d, k_rows=k_rows):
            here = tile_rows(tile)
            block = x_ref[here, :] if d == 0 else wide[d - 1, here, :]
            gate = jnp.dot(block, gate_mat[k_rows, :], preferred_element_type=jnp.float32)
            up = jnp.dot(block, up_mat[k_rows, :], preferred_element_type=jnp.float32)
            if d == 0:
                gate_acc[here, :] = gate
                up_acc[here, :] = up
            elif d != 2:
                gate_acc[here, :] += gate
                up_acc[here, :] += up
            else:
                gate = gate_acc[here, :] + gate
                up = up_acc[here, :] + up
                act[here, :] = (gate / (1.0 + jnp.exp(-gate)) * up).astype(jnp.bfloat16)
            return carry

        lax.fori_loop(0, tiles, one, 0)
    loads[2].wait()
    copies = {}
    for d in (2, 1, 3, 0):
        peer = lax.rem(me + d, size)
        out_rows = pl.ds(pl.multiple_of(peer * quarter, quarter), quarter)

        def one_part(tile, carry, d=d, out_rows=out_rows):
            here = tile_rows(tile)
            part = lax.dot_general(
                act[here, :],
                down_mat[out_rows, :],
                (((1,), (1,)), ((), ())),
                preferred_element_type=jnp.float32,
            )
            parts[d, here, :] = part.astype(jnp.bfloat16)
            return carry

        lax.fori_loop(0, tiles, one_part, 0)
        if d:
            copies[d] = send(parts.at[d], landed.at[d - 1], s2.at[d - 1], r2.at[d - 1], peer)
    for d in (1, 3, 2):
        copies[d].wait()

    def total(tile, carry):
        here = tile_rows(tile)
        summed = parts[0, here, :].astype(jnp.float32)
        for d in range(1, size):
            summed = summed + landed[d - 1, here, :].astype(jnp.float32)
        out_ref[here, :] = summed.astype(jnp.bfloat16)
        return carry

    lax.fori_loop(0, tiles, total, 0)


def expert_call(size, x, gate_mat, up_mat, down_mat):
    rows, quarter = x.shape
    vmem = pl.BlockSpec(memory_space=pltpu.VMEM)
    hbm = pl.BlockSpec(memory_space=pl.ANY)
    dma = pltpu.SemaphoreType.DMA((size - 1,))
    hidden = gate_mat.shape[1]
    return pl.pallas_call(
        lambda *refs: expert_kernel(size, *refs),
        out_shape=jax.ShapeDtypeStruct((rows, quarter), jnp.bfloat16),
        in_specs=[vmem, hbm, hbm, hbm],
        out_specs=vmem,
        scratch_shapes=[
            pltpu.VMEM(gate_mat.shape, jnp.bfloat16),
            pltpu.VMEM(up_mat.shape, jnp.bfloat16),
            pltpu.VMEM(down_mat.shape, jnp.bfloat16),
            pltpu.VMEM((size - 1, rows, quarter), jnp.bfloat16),
            pltpu.VMEM((rows, hidden), jnp.float32),
            pltpu.VMEM((rows, hidden), jnp.float32),
            pltpu.VMEM((rows, hidden), jnp.bfloat16),
            pltpu.VMEM((size, rows, quarter), jnp.bfloat16),
            pltpu.VMEM((size - 1, rows, quarter), jnp.bfloat16),
            pltpu.SemaphoreType.DMA((3,)),
            dma,
            dma,
            dma,
            dma,
        ],
        compiler_params=pltpu.CompilerParams(
            collective_id=2, has_side_effects=True, vmem_limit_bytes=40 * 1024 * 1024
        ),
        name="expert_exchange",
    )(x, gate_mat, up_mat, down_mat)


def per_device(
    residual,
    queries,
    rotated_key_rows,
    values,
    req_start,
    head_sink_logit,
    out_proj,
    mid_gain,
    router_logits,
    routes,
    placement,
    w_gate,
    w_up,
    w_down,
):
    tok_count = residual.shape[0]
    model_width = residual.shape[1]
    req_size = lax.axis_size("req")
    ffn_size = lax.axis_size("ffn")
    own_req = lax.axis_index("req")
    query_group_width = QUERY_HEADS // KEY_VALUE_HEADS
    kv_heads = rotated_key_rows.shape[1] // HEAD_SIZE
    quarter = model_width // ffn_size
    gate_mat = w_gate[0]
    up_mat = w_up[0]
    down_mat = w_down[0]
    shard_queries = queries.reshape(tok_count, kv_heads, query_group_width, HEAD_SIZE)
    local_keys = rotated_key_rows.reshape(tok_count, kv_heads, HEAD_SIZE)
    local_values = values.reshape(tok_count, kv_heads, HEAD_SIZE)
    win_span = min(16, req_size // 2)
    window = win_span * tok_count
    query_pos = own_req * tok_count + jnp.arange(tok_count, dtype=jnp.int32)
    logit_scale_factor = HEAD_SIZE ** (-0.5)

    def attend(carry_state, keys_in_block, values_in_block, key_first):
        running_max, row_total, weighted_value_sum = carry_state
        attention_logits = (
            jnp.einsum(
                "veck,uek->ecvu", shard_queries, keys_in_block, preferred_element_type=jnp.float32
            )
            * logit_scale_factor
        )
        key_pos = key_first + jnp.arange(keys_in_block.shape[0], dtype=jnp.int32)
        visible = (
            (key_pos[None, :] >= req_start[:, None])
            & (key_pos[None, :] <= query_pos[:, None])
            & (query_pos[:, None] - key_pos[None, :] < window)
        )
        attention_logits = jnp.where(visible[None, None], attention_logits, -jnp.inf)
        new_max = jnp.maximum(running_max, jnp.max(attention_logits, axis=-1))
        probs = jnp.exp(attention_logits - new_max[..., None])
        factor = jnp.exp(running_max - new_max)
        row_total = row_total * factor + jnp.sum(probs, axis=-1)
        weighted_value_sum = weighted_value_sum * factor[..., None] + jnp.einsum(
            "plyw,wpj->plyj",
            probs.astype(jnp.bfloat16),
            values_in_block,
            preferred_element_type=jnp.float32,
        )
        return (new_max, row_total, weighted_value_sum)

    initial_sink_logit = jnp.broadcast_to(
        head_sink_logit.reshape(kv_heads, query_group_width, 1),
        (kv_heads, query_group_width, tok_count),
    )
    carry_state = (
        initial_sink_logit,
        jnp.ones((kv_heads, query_group_width, tok_count), jnp.float32),
        jnp.zeros((kv_heads, query_group_width, tok_count, HEAD_SIZE), jnp.float32),
    )
    carry_state = attend(carry_state, local_keys, local_values, own_req * tok_count)
    pair_count = win_span // 2

    def pair_step(step_idx, loop_carry):
        folded, near_keys, near_values = loop_carry
        mid_keys, mid_values = step_back(near_keys, near_values)
        far_keys, far_values = step_back(mid_keys, mid_values)
        key_first = (own_req - 2 * step_idx - 2) * tok_count
        folded = attend(
            folded,
            jnp.concatenate([far_keys, mid_keys], 0),
            jnp.concatenate([far_values, mid_values], 0),
            key_first,
        )
        return (folded, far_keys, far_values)

    carry_state, unused_keys, unused_values = lax.fori_loop(
        0, pair_count, pair_step, (carry_state, local_keys, local_values)
    )
    running_max, row_total, weighted_value_sum = carry_state
    attended = (weighted_value_sum / row_total[..., None]).astype(jnp.bfloat16)
    flat_attended = jnp.transpose(attended, (2, 0, 1, 3)).reshape(tok_count, -1)
    proj = jnp.dot(
        flat_attended,
        lax.all_gather(out_proj, "req", axis=1, tiled=True),
        preferred_element_type=jnp.float32,
    )
    own_hidden, normed = norm_call(
        ffn_size, proj.astype(jnp.bfloat16), residual, mid_gain.reshape(1, model_width)
    )
    capacity = 5 * tok_count // (2 * req_size)
    flat_routes = routes.reshape(-1)
    slot_iota = jnp.arange(req_size, dtype=jnp.int32)
    dest_hot = (flat_routes[:, None] == slot_iota[None, :]).astype(jnp.int32)
    slot_depth = jnp.sum((jnp.cumsum(dest_hot, axis=0) - dest_hot) * dest_hot, axis=1)
    slot_index = flat_routes * capacity + slot_depth
    slot_pair = slot_index.reshape(tok_count, 2)
    slots = jnp.arange(req_size * capacity, dtype=jnp.int32)
    hot_slots = [
        (slot_pair[:, c][:, None] == slots[None, :]).astype(jnp.bfloat16) for c in range(2)
    ]
    send_rows = lax.dot_general(
        hot_slots[0] + hot_slots[1],
        normed,
        (((0,), (0,)), ((), ())),
        preferred_element_type=jnp.float32,
    ).astype(jnp.bfloat16)
    arrived = lax.all_to_all(
        send_rows.reshape(req_size, capacity, quarter),
        "req",
        split_axis=0,
        concat_axis=0,
        tiled=True,
    )
    summed_rows = expert_call(
        ffn_size, arrived.reshape(-1, quarter), gate_mat, up_mat, down_mat
    )
    returned = lax.all_to_all(
        summed_rows.reshape(req_size, capacity, quarter),
        "req",
        split_axis=0,
        concat_axis=0,
        tiled=True,
    ).reshape(req_size * capacity, quarter)
    expert_of = jnp.sum(dest_hot * placement[None, :], axis=1).reshape(tok_count, 2)
    expert_hot = (
        expert_of[:, :, None] == jnp.arange(EXPERTS, dtype=jnp.int32)[None, None, :]
    ).astype(jnp.float32)
    chosen = jnp.sum(router_logits[:, None, :] * expert_hot, axis=2)
    logit_peak = jnp.max(chosen, axis=1, keepdims=True)
    exp_logits = jnp.exp(chosen - logit_peak)
    gate_weights = exp_logits / jnp.sum(exp_logits, axis=1, keepdims=True)
    mixture = sum(
        jnp.dot(hot_slots[c], returned, preferred_element_type=jnp.float32)
        * gate_weights[:, c][:, None]
        for c in range(2)
    )
    return (own_hidden + mixture).astype(jnp.bfloat16)


def solution(mesh):
    in_specs = (
        P("req", None),
        P("req", "ffn"),
        P("req", "ffn"),
        P("req", "ffn"),
        P("req"),
        P("ffn"),
        P("ffn", "req"),
        P(),
        P("req", None),
        P("req", None),
        P(),
        P("req", None, "ffn"),
        P("req", None, "ffn"),
        P("req", None, "ffn"),
    )
    out_specs = P("req", "ffn")
    return jax.shard_map(
        per_device, mesh=mesh, in_specs=in_specs, out_specs=out_specs, check_vma=False
    )
```
